256 devices in a mesh: ctx: 64 (over z, x_hi, y), tp: 4 (over x_lo, core).
Axes of the slice: x: 4 (x_hi: 2, x_lo: 2; x = x_hi * 2 + x_lo), y: 4, z: 8, core: 2. Of those that a mesh axis runs over, the one named last changes fastest.
Arguments:
- hit_features: bfloat16 [24576, 1024], P('ctx', 'tp'), may hold values from -6 to 6
- segment: int32 [24576], P('ctx'), may hold values from 0 to 31, never falling along the last dimension, each value on 1 to 1537 neighbouring positions
- norm1_gain: float32 [1024], replicated, may hold values from 0.1 to 1.9
- w_qkv: bfloat16 [3, 1024, 1024], P(None, None, 'tp'), may hold values from -2 to 2
- w_out: bfloat16 [1024, 1024], P('tp'), may hold values from -0.1875 to 0.1875
- norm2_gain: float32 [1024], replicated, may hold values from 0.1 to 1.9
- w_up: bfloat16 [1024, 4096], P(None, 'tp'), may hold values from -0.1875 to 0.1875
- w_down: bfloat16 [4096, 1024], P('tp'), may hold values from -0.09375 to 0.09375
Outputs:
- layer_out: bfloat16 [24576, 1024], P('ctx', 'tp')
The draws below stay inside these ranges and needn't reach their ends.
Inputs may be any that keep to these rules, and one draw needn't show every extreme that they name: `segment`: never falls from one hit to the next; every event number below 32 appears; each event holds 1 to 1537 consecutive hits and some event holds exactly 1537.
All inputs are finite; a program needn't handle non-finite values.
Results may differ from the reference program's by a relative error of at most 0.014.
Values may be sent and summed in bfloat16 or wider, within the bound.
No kernel may reach another device: no remote copies, remote signals or barrier semaphores. Data moves between devices by JAX's collectives and lax.ppermute only.
A program may use at most 128 MiB of HBM per device.

```python
import math
import jax
import jax.numpy as jnp
import numpy as np
from jax import lax

D = 1024
HEADS = 16
HEAD_DIM = 64
FF = 4096
TOK_DEV = 384
REACH = 4
TOKENS = 24576
EVENTS = 32
EVENT_MOST = 1537
N_CTX = 64
N_TP = 4


def draw_w_qkv(key, part):
    base_key = jax.random.fold_in(jax.random.fold_in(key, 17), 0)
    weights = jax.random.normal(base_key, (3, D, D), jnp.float32) * D ** (-0.5)
    sharpen = jnp.array([1.7320508, 1.7320508, 1.0], jnp.float32)
    weights = weights * sharpen[:, None, None]
    return jnp.clip(weights, -2.0, 2.0).astype(jnp.bfloat16)


def block_levels(own_key, shape, cuts, least, high):
    level, own = 1.0, jax.random.fold_in(own_key, 6)
    for axis_at, blocks in cuts:
        heights = jnp.exp(jax.random.uniform(jax.random.fold_in(own, axis_at), (blocks,), jnp.float32, least / len(cuts), high / len(cuts)))
        level = level * jnp.repeat(heights, shape[axis_at] // blocks).reshape([-1 if axis == axis_at else 1 for axis in range(len(shape))])
    return level


def split_up(amount, total, most, lean):
    loads = [(1 << 20) // math.isqrt(grade ** lean) + 1 for grade in range(2, amount + 1)]
    surplus, given = total - most - (amount - 1), [1] * (amount - 1)
    while surplus > 0:
        free = [i for i in range(amount - 1) if given[i] < most]
        pool, left = sum([loads[i] for i in free]), surplus
        for i in free:
            more = min(most - given[i], max(1, left * loads[i] // pool), surplus)
            given[i] = given[i] + more
            surplus = surplus - more
    return np.array([most] + given)


def ragged_sizes(rng, count, total, bound, skew):
    if count == 2:
        one = jax.random.randint(rng, (), max(1, total - bound), min(bound, total - 1) + 1)
        return jnp.stack([one, total - one])
    sizes = jnp.asarray(split_up(count, total, bound, skew), jnp.int32)
    twos = (count - 1) // 2
    source_of, taker = sizes[1:1 + 2 * twos:2], sizes[2:2 + 2 * twos:2]
    room = jnp.minimum(source_of - 1, bound - taker)
    moved = jax.random.randint(jax.random.fold_in(rng, 1), (twos,), 0, 1 << 20) % (room + 1)
    sizes = sizes.at[1:1 + 2 * twos:2].set(source_of - moved).at[2:2 + 2 * twos:2].set(taker + moved)
    return sizes[jax.random.permutation(jax.random.fold_in(rng, 2), count)]


def noise(key, dims, width, bound, shards=(), kind=jnp.bfloat16):
    entries = width * jax.random.normal(key, dims, jnp.float32)
    if shards:
        entries = entries * block_levels(key, dims, shards, -0.22, 0.18)
    return jnp.clip(entries, -bound, bound).astype(kind)


def setup_inputs(seed: int = 0) -> dict:
    seeds = jax.random.split(jax.random.key(seed), 9)
    hit_features = noise(seeds[0], (TOKENS, D), 1.0, 6.0, ((0, 64), (1, 4)))
    segment = jnp.searchsorted(jnp.cumsum(ragged_sizes(seeds[1], EVENTS, TOKENS, EVENT_MOST, 2)), jnp.arange(TOKENS), side="right").astype(jnp.int32)
    norm1_gain = jnp.clip(1.0 + 0.18 * jax.random.normal(seeds[2], (D,), jnp.float32), 0.1, 1.9)
    w_qkv = draw_w_qkv(jax.random.fold_in(seeds[8], 71), 0)
    w_out = noise(seeds[4], (D, D), D ** -0.5, 0.1875, ((0, 4),))
    norm2_gain = jnp.clip(1.0 + 0.18 * jax.random.normal(seeds[5], (D,), jnp.float32), 0.1, 1.9)
    w_up = noise(seeds[6], (D, FF), D ** -0.5, 0.1875, ((1, 4),))
    w_down = noise(seeds[7], (FF, D), FF ** -0.5, 0.09375, ((0, 4),))
    return dict(hit_features=hit_features, segment=segment, norm1_gain=norm1_gain, w_qkv=w_qkv, w_out=w_out, norm2_gain=norm2_gain, w_up=w_up, w_down=w_down)


epsilon = 1e-05

def rms_scale(features, gain):
    mean_square = lax.optimization_barrier(jnp.mean(features * features, axis=-1, keepdims=True))
    return features * lax.rsqrt(mean_square + epsilon) * gain

def bf16_round(array_in):
    return lax.optimization_barrier(array_in.astype(jnp.bfloat16)).astype(jnp.float32)

def grouped_sum(left, right):
    group_width = left.shape[1] // N_TP
    running = jnp.zeros((left.shape[0], right.shape[1]), jnp.float32)
    for group_index in range(N_TP):
        column_start = group_index * group_width
        partial_product = jnp.dot(left[:, column_start:column_start + group_width], right[column_start:column_start + group_width], preferred_element_type=jnp.float32)
        running = running + bf16_round(partial_product)
    return running

def attend(queries, key_rows, value_rows, segment):
    margin = REACH * TOK_DEV
    window = (2 * REACH + 1) * TOK_DEV
    key_pad = jnp.pad(key_rows, ((margin, margin), (0, 0)))
    value_pad = jnp.pad(value_rows, ((margin, margin), (0, 0)))
    segment_pad = jnp.pad(segment, (margin, margin), constant_values=-1)

    def one_block(block_index):
        block_start = block_index * TOK_DEV
        query_block = lax.dynamic_slice_in_dim(queries, block_start, TOK_DEV, 0).astype(jnp.float32).reshape(TOK_DEV, HEADS, HEAD_DIM)
        key_block = lax.dynamic_slice_in_dim(key_pad, block_start, window, 0).astype(jnp.float32).reshape(window, HEADS, HEAD_DIM)
        value_block = lax.dynamic_slice_in_dim(value_pad, block_start, window, 0).astype(jnp.float32).reshape(window, HEADS, HEAD_DIM)
        query_event = lax.dynamic_slice_in_dim(segment, block_start, TOK_DEV, 0)
        key_event = lax.dynamic_slice_in_dim(segment_pad, block_start, window, 0)
        matches = (query_event[:, None] == key_event[None, :])[None]
        scores = jnp.einsum('qhd,khd->hqk', query_block, key_block)
        masked = jnp.where(matches, scores, -1e+30)
        row_top = lax.optimization_barrier(jnp.max(masked, axis=-1, keepdims=True))
        powered = jnp.where(matches, jnp.exp(masked - row_top), 0.0)
        row_total = lax.optimization_barrier(jnp.sum(powered, axis=-1, keepdims=True))
        weights = bf16_round(powered)
        weighted = jnp.einsum('hqk,khd->hqd', weights, value_block)
        mixed_block = jnp.transpose(weighted / row_total, (1, 0, 2)).reshape(TOK_DEV, HEADS * HEAD_DIM)
        return mixed_block.astype(jnp.bfloat16)
    blocks = lax.map(one_block, jnp.arange(N_CTX, dtype=jnp.int32))
    return blocks.reshape(TOKENS, D)

def reference(hit_features, segment, norm1_gain, w_qkv, w_out, norm2_gain, w_up, w_down):
    features = hit_features.astype(jnp.float32)
    normed = rms_scale(features, norm1_gain).astype(jnp.bfloat16)
    queries = (jnp.dot(normed, w_qkv[0], preferred_element_type=jnp.float32) * HEAD_DIM ** (-0.5)).astype(jnp.bfloat16)
    key_rows = jnp.dot(normed, w_qkv[1], preferred_element_type=jnp.float32).astype(jnp.bfloat16)
    value_rows = jnp.dot(normed, w_qkv[2], preferred_element_type=jnp.float32).astype(jnp.bfloat16)
    mixed_heads = attend(queries, key_rows, value_rows, segment)
    residual = features + grouped_sum(mixed_heads, w_out)
    normed_second = rms_scale(residual, norm2_gain).astype(jnp.bfloat16)
    hidden = jax.nn.gelu(jnp.dot(normed_second, w_up, preferred_element_type=jnp.float32), approximate=False).astype(jnp.bfloat16)
    return (residual + grouped_sum(hidden, w_down)).astype(jnp.bfloat16)
```

```python
import jax
import jax.numpy as jnp
from jax import lax
from jax.experimental import pallas as pl
from jax.experimental.pallas import tpu as pltpu
from jax.sharding import Mesh, PartitionSpec as P

HEAD_DIM = 64
epsilon = 1e-05
neg_fill = -1e30
AXES = ("z", "xh", "y", "xl", "core")
CTX = ("z", "xh", "y")
TP = ("xl", "core")
SIZES = (8, 2, 4, 2, 2)
TAG_ROWS = 16


def flat(place):
    index = 0
    for size, at in zip(SIZES, place):
        index = index * size + at
    return index


def every_place():
    for index in range(256):
        place = []
        for size in reversed(SIZES):
            place.append(index % size)
            index //= size
        yield tuple(reversed(place))


def send(block, move):
    route = []
    for place in every_place():
        target = move(*place)
        if target is not None:
            route.append((flat(place), flat(target)))
    return lax.ppermute(block, AXES, route)


def to_y(distance):
    return lambda z, xh, y, xl, c: (z, xh, (y + distance) % 4, xl, c)


def to_super(distance):
    def move(z, xh, y, xl, c):
        at = 2 * z + xh + distance
        return (at // 2, at % 2, y, xl, c) if 0 <= at < 16 else None

    return move


def to_core(z, xh, y, xl, c):
    return (z, xh, y, xl, 1 - c)


def to_chip(z, xh, y, xl, c):
    return (z, xh, y, 1 - xl, c)


def params(**more):
    return pltpu.CompilerParams(vmem_limit_bytes=56 << 20, **more)


SMEM = pl.BlockSpec(memory_space=pltpu.SMEM)
VMEM = pl.BlockSpec(memory_space=pltpu.VMEM)


def project_body(place, shards, segment, gain, weights, *rest):
    outs, (normed, heads) = rest[:8], rest[8:]
    rows = shards.shape[1]
    total = jnp.zeros((rows, 1), jnp.float32)
    for j in range(4):
        part = shards[j].astype(jnp.float32)
        total = total + jnp.sum(part * part, axis=-1, keepdims=True)
    scale = lax.rsqrt(total * (1.0 / 1024) + epsilon)
    for j in range(4):
        part = shards[j].astype(jnp.float32)
        at = slice(256 * j, 256 * (j + 1))
        normed[:, at] = (part * scale * gain[:, at]).astype(jnp.bfloat16)
    for c in range(3):
        out = jnp.dot(normed[...], weights[c], preferred_element_type=jnp.float32)
        if c == 0:
            out = out * HEAD_DIM ** (-0.5)
        turned = out.T.astype(jnp.bfloat16)
        for h in range(4):
            heads[h, 64 * c : 64 * (c + 1), :] = turned[64 * h : 64 * (h + 1)]
    tag = jnp.broadcast_to((segment[...] + 1).astype(jnp.float32), (TAG_ROWS, rows)).astype(jnp.bfloat16)
    y = place[0]
    for d in range(4):
        h = lax.rem(y + d, 4)
        outs[d][...] = heads[h, 0:64, :]
        outs[4 + d][0:128, :] = heads[h, 64:192, :]
        outs[4 + d][128 : 128 + TAG_ROWS, :] = tag


def project(place, shards, segment, gain, weights):
    rows = shards.shape[1]
    out = [jax.ShapeDtypeStruct((64, rows), jnp.bfloat16)] * 4
    out += [jax.ShapeDtypeStruct((128 + TAG_ROWS, rows), jnp.bfloat16)] * 4
    return pl.pallas_call(
        project_body,
        name="project",
        out_shape=out,
        in_specs=[SMEM, VMEM, VMEM, VMEM, VMEM],
        out_specs=[VMEM] * 8,
        scratch_shapes=[
            pltpu.VMEM((rows, 1024), jnp.bfloat16),
            pltpu.VMEM((4, 192, rows), jnp.bfloat16),
        ],
        compiler_params=params(),
    )(place, shards, segment, gain, weights)


def attend_body(chunks, first, last, *refs):
    queries, query_sides, sides = refs[:4], refs[4:8], refs[8 : 8 + chunks]
    refs = refs[8 + chunks :]
    if not first:
        state, refs = refs[:3], refs[3:]
    outs, refs = (refs[:4], refs[4:]) if last else (refs[:3], refs[3:])
    if last:
        top, total, mixed = refs[:3]
        refs = refs[3:]
    else:
        top, total, mixed = outs
    query_all, query_tag, key_all, value_all, key_tag, query_low, query_high, key_low, key_high = refs
    rows = 384
    for i in range(4):
        query_all[i] = queries[i][...]
        tag = query_sides[i][128:129, :].astype(jnp.float32)
        query_tag[i] = tag
        query_low[i] = jnp.min(tag)
        query_high[i] = jnp.max(tag)
    for j in range(chunks):
        side = sides[j][...].astype(jnp.float32)
        key_all[j] = side[0:64].T.astype(jnp.bfloat16)
        value_all[j] = sides[j][64:128, :]
        key_tag[j] = side[128:136].T[:, 0:1]
        tag = side[128:129]
        key_low[j] = jnp.min(tag)
        key_high[j] = jnp.max(tag)
    if first:
        top[...] = jnp.full(top.shape, neg_fill, jnp.float32)
        total[...] = jnp.zeros(total.shape, jnp.float32)
        mixed[...] = jnp.zeros(mixed.shape, jnp.float32)
    else:
        top[...] = state[0][...]
        total[...] = state[1][...]
        mixed[...] = state[2][...]

    def pair(index, carry):
        i = index // chunks
        j = lax.rem(index, chunks)
        meets = (query_low[i] <= key_high[j]) & (key_low[j] <= query_high[i])

        @pl.when(meets)
        def _():
            scores = jnp.dot(key_all[j], query_all[i], preferred_element_type=jnp.float32)
            matches = key_tag[j] == query_tag[i]
            masked = jnp.where(matches, scores, neg_fill)
            old_top = top[i]
            new_top = jnp.maximum(old_top, jnp.max(masked, axis=0, keepdims=True))
            powered = jnp.where(matches, jnp.exp(masked - new_top), 0.0)
            rescale = jnp.exp(old_top - new_top)
            total[i] = total[i] * rescale + jnp.sum(powered, axis=0, keepdims=True)
            mixed[i] = mixed[i] * rescale + jnp.dot(
                value_all[j], powered.astype(jnp.bfloat16), preferred_element_type=jnp.float32
            )
            top[i] = new_top

        return carry

    lax.fori_loop(0, 4 * chunks, pair, 0)
    if last:
        for i in range(4):
            outs[i][...] = (mixed[i] / total[i]).astype(jnp.bfloat16)


def attend(queries, query_sides, sides, state, last):
    chunks = len(sides)
    rows = queries[0].shape[1]
    first = state is None
    shapes = [(4, 1, rows), (4, 1, rows), (4, 64, rows)]
    scratch = []
    if last:
        out = [jax.ShapeDtypeStruct((64, rows), jnp.bfloat16)] * 4
        scratch = [pltpu.VMEM(s, jnp.float32) for s in shapes]
    else:
        out = [jax.ShapeDtypeStruct(s, jnp.float32) for s in shapes]
    scratch += [
        pltpu.VMEM((4, 64, rows), jnp.bfloat16),
        pltpu.VMEM((4, 1, rows), jnp.float32),
        pltpu.VMEM((chunks, rows, 64), jnp.bfloat16),
        pltpu.VMEM((chunks, 64, rows), jnp.bfloat16),
        pltpu.VMEM((chunks, rows, 1), jnp.float32),
        pltpu.SMEM((4,), jnp.float32),
        pltpu.SMEM((4,), jnp.float32),
        pltpu.SMEM((chunks,), jnp.float32),
        pltpu.SMEM((chunks,), jnp.float32),
    ]
    args = list(queries) + list(query_sides) + list(sides) + ([] if first else list(state))

    def body(*refs):
        attend_body(chunks, first, last, *refs)

    return pl.pallas_call(
        body,
        name="attend_far" if last else "attend_near",
        out_shape=out,
        in_specs=[VMEM] * len(args),
        out_specs=[VMEM] * len(out),
        scratch_shapes=scratch,
        compiler_params=params(),
    )(*args)


def columns(index):
    return pl.ds(pl.multiple_of(index * 256, 256), 256)


def output_body(place, first, second, third, fourth, weights, keep, give, heads):
    y, c = place[0], place[2]
    for d, chunk in enumerate((first, second, third, fourth)):
        heads[lax.rem(y - d + 4, 4)] = chunk[...].astype(jnp.float32).T.astype(jnp.bfloat16)
    mixed = jnp.concatenate([heads[h] for h in range(4)], axis=1)
    for j in range(2):
        at = slice(256 * j, 256 * (j + 1))
        give[:, at] = jnp.dot(
            mixed, weights[:, columns(2 * j + 1 - c)], preferred_element_type=jnp.float32
        ).astype(jnp.bfloat16)
    for j in range(2):
        at = slice(256 * j, 256 * (j + 1))
        keep[:, at] = jnp.dot(
            mixed, weights[:, columns(2 * j + c)], preferred_element_type=jnp.float32
        ).astype(jnp.bfloat16)


def output(place, chunks, weights):
    rows = chunks[0].shape[1]
    return pl.pallas_call(
        output_body,
        name="output",
        out_shape=[jax.ShapeDtypeStruct((rows, 512), jnp.bfloat16)] * 2,
        in_specs=[SMEM] + [VMEM] * 5,
        out_specs=[VMEM] * 2,
        scratch_shapes=[pltpu.VMEM((4, rows, 64), jnp.bfloat16)],
        compiler_params=params(),
    )(place, *chunks, weights)


def feed_body(place, shards, mine, theirs, gain, w_up, w_down, keep, give, share, residual, normed):
    x, c = place[1], place[2]
    rows = shards.shape[1]
    total = jnp.zeros((rows, 1), jnp.float32)
    for j in range(2):
        at = slice(256 * j, 256 * (j + 1))
        for source, b in ((mine, 2 * j + c), (theirs, 2 * j + 1 - c)):
            part = shards[b].astype(jnp.float32) + source[:, at].astype(jnp.float32)
            residual[b] = part
            total = total + jnp.sum(part * part, axis=-1, keepdims=True)
    scale = lax.rsqrt(total * (1.0 / 1024) + epsilon)
    for b in range(4):
        at = slice(256 * b, 256 * (b + 1))
        normed[:, at] = (residual[b] * scale * gain[:, at]).astype(jnp.bfloat16)
    share[...] = residual[2 * x + c]
    raised = jnp.dot(normed[...], w_up[...], preferred_element_type=jnp.float32)
    hidden = (raised * (1.0 + lax.erf(raised * 0.7071067811865476)) * 0.5).astype(jnp.bfloat16)
    for j in range(2):
        at = slice(256 * j, 256 * (j + 1))
        give[:, at] = jnp.dot(
            hidden, w_down[:, columns(2 * j + 1 - c)], preferred_element_type=jnp.float32
        ).astype(jnp.bfloat16)
    for j in range(2):
        at = slice(256 * j, 256 * (j + 1))
        keep[:, at] = jnp.dot(
            hidden, w_down[:, columns(2 * j + c)], preferred_element_type=jnp.float32
        ).astype(jnp.bfloat16)


def feed(place, shards, mine, theirs, gain, w_up, w_down):
    rows = shards.shape[1]
    return pl.pallas_call(
        feed_body,
        name="feed",
        out_shape=[
            jax.ShapeDtypeStruct((rows, 512), jnp.bfloat16),
            jax.ShapeDtypeStruct((rows, 512), jnp.bfloat16),
            jax.ShapeDtypeStruct((rows, 256), jnp.float32),
        ],
        in_specs=[SMEM] + [VMEM] * 6,
        out_specs=[VMEM] * 3,
        scratch_shapes=[
            pltpu.VMEM((4, rows, 256), jnp.float32),
            pltpu.VMEM((rows, 1024), jnp.bfloat16),
        ],
        compiler_params=params(),
    )(place, shards, mine, theirs, gain, w_up, w_down)


def split_body(place, keep, got, own, give):
    x = place[1]
    for j in range(2):
        at = slice(256 * j, 256 * (j + 1))
        summed = keep[:, at].astype(jnp.float32) + got[:, at].astype(jnp.float32)

        @pl.when(x == j)
        def _():
            own[...] = summed

        @pl.when(x != j)
        def _():
            give[...] = summed.astype(jnp.bfloat16)


def split(place, keep, got):
    rows = keep.shape[0]
    return pl.pallas_call(
        split_body,
        name="split",
        out_shape=[
            jax.ShapeDtypeStruct((rows, 256), jnp.float32),
            jax.ShapeDtypeStruct((rows, 256), jnp.bfloat16),
        ],
        in_specs=[SMEM] + [VMEM] * 2,
        out_specs=[VMEM] * 2,
        compiler_params=params(),
    )(place, keep, got)


def shards(hit_features, segment, norm1_gain, w_qkv, w_out, norm2_gain, w_up, w_down):
    place = jnp.stack([lax.axis_index("y"), lax.axis_index("xl"), lax.axis_index("core")]).astype(jnp.int32)
    features = lax.all_gather(hit_features, TP, axis=0, tiled=False)
    made = project(place, features, segment[None, :], norm1_gain[None, :], w_qkv)
    queries, sides = [made[0]], [made[4]]
    for d in range(1, 4):
        sides.append(send(made[4 + d], to_y(d)))
    for d in range(1, 4):
        queries.append(send(made[d], to_y(d)))
    far = []
    for d in range(4):
        far.append(send(sides[d], to_super(1)))
        far.append(send(sides[d], to_super(-1)))
    state = attend(queries, sides, sides, None, False)
    mixed = attend(queries, sides, far, state, True)
    chunks = [mixed[0]] + [None] * 3
    for d in range(1, 4):
        chunks[(4 - d) % 4] = send(mixed[d], to_y(-d))
    keep, give = output(place, chunks, w_out)
    half = keep.astype(jnp.float32) + send(give, to_core).astype(jnp.float32)
    half = half.astype(jnp.bfloat16)
    other = send(half, to_chip)
    mine = half.astype(jnp.float32) + other.astype(jnp.float32)
    theirs = send(mine.astype(jnp.bfloat16), to_core)
    keep, give, share = feed(place, features, mine, theirs, norm2_gain[None, :], w_up, w_down)
    own, give = split(place, keep, send(give, to_core))
    got = send(give, to_chip)
    return (share + own + got.astype(jnp.float32)).astype(jnp.bfloat16)


def solution(mesh):
    fine = Mesh(mesh.devices.reshape(SIZES), AXES)
    return jax.shard_map(
        shards,
        mesh=fine,
        in_specs=(
            P(CTX, TP),
            P(CTX),
            P(),
            P(None, None, TP),
            P(TP, None),
            P(),
            P(None, TP),
            P(TP, None),
        ),
        out_specs=P(CTX, TP),
        check_vma=False,
    )
```

```python
import jax
import jax.numpy as jnp
from jax import lax
from jax.experimental import pallas as pl
from jax.experimental.pallas import tpu as pltpu
from jax.sharding import Mesh, PartitionSpec as P

HEAD_DIM = 64
epsilon = 1e-05
neg_fill = -1e30
AXES = ("z", "xh", "y", "xl", "core")
CTX = ("z", "xh", "y")
TP = ("xl", "core")
SIZES = (8, 2, 4, 2, 2)
TAG_ROWS = 8


def flat(place):
    index = 0
    for size, at in zip(SIZES, place):
        index = index * size + at
    return index


def every_place():
    for index in range(256):
        place = []
        for size in reversed(SIZES):
            place.append(index % size)
            index //= size
        yield tuple(reversed(place))


def send(block, move):
    route = []
    for place in every_place():
        target = move(*place)
        if target is not None:
            route.append((flat(place), flat(target)))
    return lax.ppermute(block, AXES, route)


def to_y(distance):
    return lambda z, xh, y, xl, c: (z, xh, (y + distance) % 4, xl, c)


def to_super(distance):
    def move(z, xh, y, xl, c):
        at = 2 * z + xh + distance
        return (at // 2, at % 2, y, xl, c) if 0 <= at < 16 else None

    return move


def to_core(z, xh, y, xl, c):
    return (z, xh, y, xl, 1 - c)


def to_chip(z, xh, y, xl, c):
    return (z, xh, y, 1 - xl, c)


def params(mib):
    return pltpu.CompilerParams(vmem_limit_bytes=mib << 20)


SMEM = pl.BlockSpec(memory_space=pltpu.SMEM)
VMEM = pl.BlockSpec(memory_space=pltpu.VMEM)


def group_orders(x, c):
    return (2 * x + c, 2 * x + 1 - c, 2 * (1 - x) + c, 2 * (1 - x) + 1 - c)


def project_body(place, own, near, far, both, segment, gain, weights, *rest):
    outs, (features, normed, heads) = rest[:4], rest[4:]
    y = place[0]
    rows = own.shape[0]
    total = jnp.zeros((rows, 1), jnp.float32)
    for source, at in zip((own, near, far, both), group_orders(place[1], place[2])):
        part = source[...].astype(jnp.float32)
        total = total + jnp.sum(part * part, axis=-1, keepdims=True)
        features[at] = source[...]
    scale = lax.rsqrt(total * (1.0 / 1024) + epsilon)
    for j in range(4):
        at = slice(256 * j, 256 * (j + 1))
        normed[:, at] = (features[j].astype(jnp.float32) * scale * gain[:, at]).astype(jnp.bfloat16)
    for c in range(3):
        out = jnp.dot(normed[...], weights[c], preferred_element_type=jnp.float32)
        if c == 0:
            out = out * HEAD_DIM ** (-0.5)
        turned = out.T.astype(jnp.bfloat16)
        for h in range(4):
            heads[h, 64 * c : 64 * (c + 1), :] = turned[64 * h : 64 * (h + 1)]
    tag = jnp.broadcast_to((segment[...] + 1).astype(jnp.float32), (TAG_ROWS, rows)).astype(jnp.bfloat16)
    for d in range(4):
        outs[d][0:192, :] = heads[lax.rem(y + d, 4)]
        outs[d][192 : 192 + TAG_ROWS, :] = tag


def project(place, parts, segment, gain, weights):
    rows = parts[0].shape[0]
    return pl.pallas_call(
        project_body,
        name="project",
        out_shape=[jax.ShapeDtypeStruct((192 + TAG_ROWS, rows), jnp.bfloat16)] * 4,
        in_specs=[SMEM] + [VMEM] * 7,
        out_specs=[VMEM] * 4,
        scratch_shapes=[
            pltpu.VMEM((4, rows, 256), jnp.bfloat16),
            pltpu.VMEM((rows, 1024), jnp.bfloat16),
            pltpu.VMEM((4, 192, rows), jnp.bfloat16),
        ],
        compiler_params=params(20),
    )(place, *parts, segment, gain, weights)


def pack_body(first, second, third, fourth, out):
    for d, source in enumerate((first, second, third, fourth)):
        out[d] = source[64 : 192 + TAG_ROWS, :]


def pack(payloads):
    rows = payloads[0].shape[1]
    return pl.pallas_call(
        pack_body,
        name="pack",
        out_shape=jax.ShapeDtypeStruct((4, 128 + TAG_ROWS, rows), jnp.bfloat16),
        in_specs=[VMEM] * 4,
        out_specs=VMEM,
        compiler_params=params(8),
    )(*payloads)


def attend_body(first, *refs):
    payloads, refs = refs[:4], refs[4:]
    chunks = 4 if first else 8
    if first:
        sides = [p.at[64 : 192 + TAG_ROWS, :] for p in payloads]
        top, mixed = refs[:2]
        refs = refs[2:]
    else:
        sides = [refs[k].at[d] for k in range(2) for d in range(4)]
        top_in, mixed_in = refs[2:4]
        outs = refs[4:8]
        top, mixed = refs[8:10]
        refs = refs[10:]
    query_tag, key_all, value_all, key_tag, query_low, query_high, key_low, key_high = refs
    rows = payloads[0].shape[1]
    for i in range(4):
        tag = payloads[i][192 : 192 + TAG_ROWS, :].astype(jnp.float32)[0:1]
        query_tag[i] = tag
        query_low[i] = jnp.min(tag)
        query_high[i] = jnp.max(tag)
    all_low = jnp.minimum(jnp.minimum(query_low[0], query_low[1]), jnp.minimum(query_low[2], query_low[3]))
    all_high = jnp.maximum(jnp.maximum(query_high[0], query_high[1]), jnp.maximum(query_high[2], query_high[3]))
    for j in range(chunks):
        tags = sides[j][128 : 128 + TAG_ROWS, :].astype(jnp.float32)
        low, high = jnp.min(tags), jnp.max(tags)
        key_low[j] = low
        key_high[j] = high

        @pl.when((all_low <= high) & (low <= all_high))
        def _():
            key_all[j] = sides[j][0:64, :].astype(jnp.float32).T.astype(jnp.bfloat16)
            value_all[j, 0:64] = sides[j][64:128, :]
            value_all[j, 64:80] = jnp.ones((16, rows), jnp.bfloat16)
            key_tag[j] = tags.T[:, 0:1]

    if first:
        top[...] = jnp.full(top.shape, neg_fill, jnp.float32)
        mixed[...] = jnp.zeros(mixed.shape, jnp.float32)
    else:
        top[...] = top_in[...]
        mixed[...] = mixed_in[...]

    for i in range(4):

        def pair(j, carry):
            meets = (query_low[i] <= key_high[j]) & (key_low[j] <= query_high[i])

            @pl.when(meets)
            def _():
                scores = jnp.dot(key_all[j], payloads[i][0:64, :], preferred_element_type=jnp.float32)
                masked = jnp.where(key_tag[j] == query_tag[i], scores, 2 * neg_fill)
                old_top = top[i]
                new_top = jnp.maximum(old_top, jnp.max(masked, axis=0, keepdims=True))
                powered = jnp.exp(masked - new_top).astype(jnp.bfloat16)
                rescale = jnp.exp(old_top - new_top)
                mixed[i] = mixed[i] * rescale + jnp.dot(value_all[j], powered, preferred_element_type=jnp.float32)
                top[i] = new_top

            return carry

        lax.fori_loop(0, chunks, pair, 0)
        if not first:
            outs[i][...] = (mixed[i, 0:64] / mixed[i, 64:65]).astype(jnp.bfloat16)


def attend(payloads, sides, state):
    rows = payloads[0].shape[1]
    first = state is None
    chunks = 4 if first else 8
    shapes = [(4, 1, rows), (4, 80, rows)]
    scratch = []
    if first:
        args = list(payloads)
        out = [jax.ShapeDtypeStruct(s, jnp.float32) for s in shapes]
    else:
        args = list(payloads) + list(sides) + list(state)
        out = [jax.ShapeDtypeStruct((64, rows), jnp.bfloat16)] * 4
        scratch = [pltpu.VMEM(s, jnp.float32) for s in shapes]
    scratch += [
        pltpu.VMEM((4, 1, rows), jnp.float32),
        pltpu.VMEM((chunks, rows, 64), jnp.bfloat16),
        pltpu.VMEM((chunks, 80, rows), jnp.bfloat16),
        pltpu.VMEM((chunks, rows, 1), jnp.float32),
        pltpu.SMEM((4,), jnp.float32),
        pltpu.SMEM((4,), jnp.float32),
        pltpu.SMEM((chunks,), jnp.float32),
        pltpu.SMEM((chunks,), jnp.float32),
    ]

    def body(*refs):
        attend_body(first, *refs)

    return pl.pallas_call(
        body,
        name="attend_near" if first else "attend_far",
        out_shape=out,
        in_specs=[VMEM] * len(args),
        out_specs=[VMEM] * len(out),
        scratch_shapes=scratch,
        compiler_params=params(20),
    )(*args)


def gather_body(place, first, second, third, fourth, out):
    y = place[0]
    for d, chunk in enumerate((first, second, third, fourth)):
        out[lax.rem(y - d + 4, 4)] = chunk[...]


def gather_heads(place, chunks):
    rows = chunks[0].shape[1]
    return pl.pallas_call(
        gather_body,
        name="gather_heads",
        out_shape=jax.ShapeDtypeStruct((4, 64, rows), jnp.bfloat16),
        in_specs=[SMEM] + [VMEM] * 4,
        out_specs=VMEM,
        compiler_params=params(8),
    )(place, *chunks)


def columns(index):
    return pl.ds(pl.multiple_of(index * 256, 256), 256)


def feed_body(place, *refs):
    parts, mixed, outers, (gain, w_up, w_down), outs, scratch = (
        refs[:4], refs[4:8], refs[8:12], refs[12:15], refs[15:20], refs[20:]
    )
    far_keep, far_give, near_keep, near_give, share = outs
    features, residual, normed = scratch
    x, c = place[1], place[2]
    rows = parts[0].shape[0]
    for source, at in zip(parts, group_orders(x, c)):
        features[at] = source[...]
    attn = jnp.zeros((rows, 1024), jnp.float32)
    for heads, outer in zip(mixed, outers):
        turned = heads[...].reshape(256, rows).astype(jnp.float32).T.astype(jnp.bfloat16)
        attn = attn + jnp.dot(turned, outer[...], preferred_element_type=jnp.float32)
    total = jnp.zeros((rows, 1), jnp.float32)
    for b in range(4):
        part = features[b].astype(jnp.float32) + attn[:, 256 * b : 256 * (b + 1)]
        residual[b] = part
        total = total + jnp.sum(part * part, axis=-1, keepdims=True)
    scale = lax.rsqrt(total * (1.0 / 1024) + epsilon)
    for b in range(4):
        at = slice(256 * b, 256 * (b + 1))
        normed[:, at] = (residual[b] * scale * gain[:, at]).astype(jnp.bfloat16)
    share[...] = residual[2 * x + c]
    raised = jnp.dot(normed[...], w_up[...], preferred_element_type=jnp.float32)
    hidden = (raised * (1.0 + lax.erf(raised * 0.7071067811865476)) * 0.5).astype(jnp.bfloat16)
    near_at, pair_at, far_at, both_at = group_orders(x, c)
    for out, at in ((far_give, both_at), (far_keep, far_at), (near_give, pair_at), (near_keep, near_at)):
        out[...] = jnp.dot(hidden, w_down[:, columns(at)], preferred_element_type=jnp.float32).astype(jnp.bfloat16)


def feed(place, parts, mixed, outers, gain, w_up, w_down):
    rows = parts[0].shape[0]
    return pl.pallas_call(
        feed_body,
        name="feed",
        out_shape=[jax.ShapeDtypeStruct((rows, 256), jnp.bfloat16)] * 4
        + [jax.ShapeDtypeStruct((rows, 256), jnp.float32)],
        in_specs=[SMEM] + [VMEM] * 15,
        out_specs=[VMEM] * 5,
        scratch_shapes=[
            pltpu.VMEM((4, rows, 256), jnp.bfloat16),
            pltpu.VMEM((4, rows, 256), jnp.float32),
            pltpu.VMEM((rows, 1024), jnp.bfloat16),
        ],
        compiler_params=params(32),
    )(place, *parts, *mixed, *outers, gain, w_up, w_down)


def everyone(block):
    far = send(block, to_chip)
    return [block, send(block, to_core), far, send(far, to_core)]


def shards(hit_features, segment, norm1_gain, w_qkv, w_out, norm2_gain, w_up, w_down):
    place = jnp.stack([lax.axis_index("y"), lax.axis_index("xl"), lax.axis_index("core")]).astype(jnp.int32)
    parts = everyone(hit_features)
    made = project(place, parts, segment[None, :], norm1_gain[None, :], w_qkv)
    payloads = [made[0]] + [send(made[d], to_y(d)) for d in range(1, 4)]
    w_late, _ = lax.optimization_barrier((w_out, made[0]))
    sides = pack(payloads)
    far = [send(sides, to_super(1)), send(sides, to_super(-1))]
    state = attend(payloads, None, None)
    outers = everyone(w_late)
    mixed = attend(payloads, far, state)
    chunks = [mixed[0]] + [None] * 3
    for d in range(1, 4):
        chunks[(4 - d) % 4] = send(mixed[d], to_y(-d))
    heads = everyone(gather_heads(place, chunks))
    far_keep, far_give, near_keep, near_give, share = feed(
        place, parts, heads, outers, norm2_gain[None, :], w_up, w_down
    )
    summed = far_keep.astype(jnp.float32) + send(far_give, to_core).astype(jnp.float32)
    got = send(summed.astype(jnp.bfloat16), to_chip)
    own = share + near_keep.astype(jnp.float32) + send(near_give, to_core).astype(jnp.float32)
    return (own + got.astype(jnp.float32)).astype(jnp.bfloat16)


def solution(mesh):
    fine = Mesh(mesh.devices.reshape(SIZES), AXES)
    return jax.shard_map(
        shards,
        mesh=fine,
        in_specs=(
            P(CTX, TP),
            P(CTX),
            P(),
            P(None, None, TP),
            P(TP, None),
            P(),
            P(None, TP),
            P(TP, None),
        ),
        out_specs=P(CTX, TP),
        check_vma=False,
    )
```

```python
import jax
import jax.numpy as jnp
from jax import lax
from jax.experimental import pallas as pl
from jax.experimental.pallas import tpu as pltpu
from jax.sharding import Mesh, PartitionSpec as P


HEAD_DIM = 64
epsilon = 1e-05
neg_fill = -1e30
AXES = ("z", "xh", "y", "xl", "core")
CTX = ("z", "xh", "y")
TP = ("xl", "core")
SIZES = (8, 2, 4, 2, 2)
TAG_ROWS = 8


def flat(place):
    index = 0
    for size, at in zip(SIZES, place):
        index = index * size + at
    return index


def every_place():
    for index in range(256):
        place = []
        for size in reversed(SIZES):
            place.append(index % size)
            index //= size
        yield tuple(reversed(place))


def send(block, move):
    route = []
    for place in every_place():
        target = move(*place)
        if target is not None:
            route.append((flat(place), flat(target)))
    return lax.ppermute(block, AXES, route)


def to_y(distance):
    return lambda z, xh, y, xl, c: (z, xh, (y + distance) % 4, xl, c)


def to_super(distance):
    def move(z, xh, y, xl, c):
        at = 2 * z + xh + distance
        return (at // 2, at % 2, y, xl, c) if 0 <= at < 16 else None

    return move


def to_core(z, xh, y, xl, c):
    return (z, xh, y, xl, 1 - c)


def to_chip(z, xh, y, xl, c):
    return (z, xh, y, 1 - xl, c)


def params(mib):
    return pltpu.CompilerParams(vmem_limit_bytes=mib << 20)


SMEM = pl.BlockSpec(memory_space=pltpu.SMEM)
VMEM = pl.BlockSpec(memory_space=pltpu.VMEM)
HBM = pl.BlockSpec(memory_space=pltpu.HBM)


def group_orders(x, c):
    return (2 * x + c, 2 * x + 1 - c, 2 * (1 - x) + c, 2 * (1 - x) + 1 - c)


def stage_body(weights, own, segment, weights_out, own_out, tags, sems):
    copies = [
        pltpu.make_async_copy(weights, weights_out, sems.at[0]),
        pltpu.make_async_copy(own, own_out, sems.at[1]),
    ]
    for copy in copies:
        copy.start()
    tag = (segment[...] + 1).astype(jnp.float32)
    tags[...] = jnp.broadcast_to(tag, tags.shape).astype(jnp.bfloat16)
    for copy in copies:
        copy.wait()


def stage(weights, own, segment):
    return pl.pallas_call(
        stage_body,
        name="stage",
        out_shape=[
            jax.ShapeDtypeStruct(weights.shape, weights.dtype),
            jax.ShapeDtypeStruct(own.shape, own.dtype),
            jax.ShapeDtypeStruct((TAG_ROWS, own.shape[0]), jnp.bfloat16),
        ],
        in_specs=[HBM, HBM, VMEM],
        out_specs=[VMEM] * 3,
        scratch_shapes=[pltpu.SemaphoreType.DMA((2,))],
        compiler_params=params(8),
    )(weights, own, segment)


def project_body(place, own, near, far, both, tags, gain, weights, *rest):
    queries, sides, (features, normed, heads) = rest[:4], rest[4:8], rest[8:]
    y = place[0]
    rows = own.shape[0]
    total = jnp.zeros((rows, 1), jnp.float32)
    for source, at in zip((own, near, far, both), group_orders(place[1], place[2])):
        part = source[...].astype(jnp.float32)
        total = total + jnp.sum(part * part, axis=-1, keepdims=True)
        features[at] = source[...]
    scale = lax.rsqrt(total * (1.0 / 1024) + epsilon)
    for j in range(4):
        at = slice(256 * j, 256 * (j + 1))
        normed[:, at] = (features[j].astype(jnp.float32) * scale * gain[:, at]).astype(jnp.bfloat16)
    for c in range(3):
        out = jnp.dot(normed[...], weights[c], preferred_element_type=jnp.float32)
        if c == 0:
            out = out * HEAD_DIM ** (-0.5)
        turned = out.T.astype(jnp.bfloat16)
        for h in range(4):
            heads[h, 64 * c : 64 * (c + 1), :] = turned[64 * h : 64 * (h + 1)]
    for d in range(4):
        h = lax.rem(y + d, 4)
        queries[d][...] = heads[h, 0:64, :]
        sides[d][0:128, :] = heads[h, 64:192, :]
        sides[d][128 : 128 + TAG_ROWS, :] = tags[...]


def project(place, parts, tags, gain, weights):
    rows = parts[0].shape[0]
    return pl.pallas_call(
        project_body,
        name="project",
        out_shape=[jax.ShapeDtypeStruct((64, rows), jnp.bfloat16)] * 4
        + [jax.ShapeDtypeStruct((128 + TAG_ROWS, rows), jnp.bfloat16)] * 4,
        in_specs=[SMEM] + [VMEM] * 7,
        out_specs=[VMEM] * 8,
        scratch_shapes=[
            pltpu.VMEM((4, rows, 256), jnp.bfloat16),
            pltpu.VMEM((rows, 1024), jnp.bfloat16),
            pltpu.VMEM((4, 192, rows), jnp.bfloat16),
        ],
        compiler_params=params(20),
    )(place, *parts, tags, gain, weights)


def pack_body(first, second, third, fourth, out):
    for d, source in enumerate((first, second, third, fourth)):
        out[d] = source[...]


def pack(payloads):
    rows = payloads[0].shape[1]
    return pl.pallas_call(
        pack_body,
        name="pack",
        out_shape=jax.ShapeDtypeStruct((4, 128 + TAG_ROWS, rows), jnp.bfloat16),
        in_specs=[VMEM] * 4,
        out_specs=VMEM,
        compiler_params=params(8),
    )(*payloads)


def attend_body(first, last, *refs):
    queries, own_sides, sides, refs = refs[:4], refs[4], refs[5], refs[6:]
    if not first:
        top_in, mixed_in = refs[:2]
        refs = refs[2:]
    if last:
        outs, refs = refs[:4], refs[4:]
    top, mixed = refs[:2]
    query_tag, key_all, value_all, key_tag, query_low, query_high, key_low, key_high = refs[2:]
    rows = sides.shape[2]
    for i in range(4):
        tag = own_sides[i, 128 : 128 + TAG_ROWS, :].astype(jnp.float32)[0:1]
        query_tag[i] = tag
        query_low[i] = jnp.min(tag)
        query_high[i] = jnp.max(tag)
    all_low = jnp.minimum(jnp.minimum(query_low[0], query_low[1]), jnp.minimum(query_low[2], query_low[3]))
    all_high = jnp.maximum(jnp.maximum(query_high[0], query_high[1]), jnp.maximum(query_high[2], query_high[3]))
    for j in range(4):
        tags = sides[j, 128 : 128 + TAG_ROWS, :].astype(jnp.float32)
        low, high = jnp.min(tags), jnp.max(tags)
        key_low[j] = low
        key_high[j] = high

        @pl.when((all_low <= high) & (low <= all_high))
        def _():
            key_all[j] = sides[j, 0:64, :].astype(jnp.float32).T.astype(jnp.bfloat16)
            value_all[j, 0:64] = sides[j, 64:128, :]
            value_all[j, 64:80] = jnp.ones((16, rows), jnp.bfloat16)
            key_tag[j] = tags.T[:, 0:1]

    if first:
        top[...] = jnp.full(top.shape, neg_fill, jnp.float32)
        mixed[...] = jnp.zeros(mixed.shape, jnp.float32)
    else:
        top[...] = top_in[...]
        mixed[...] = mixed_in[...]

    for i in range(4):

        def pair(j, carry):
            meets = (query_low[i] <= key_high[j]) & (key_low[j] <= query_high[i])

            @pl.when(meets)
            def _():
                scores = jnp.dot(key_all[j], queries[i][...], preferred_element_type=jnp.float32)
                masked = jnp.where(key_tag[j] == query_tag[i], scores, 2 * neg_fill)
                old_top = top[i]
                new_top = jnp.maximum(old_top, jnp.max(masked, axis=0, keepdims=True))
                powered = jnp.exp(masked - new_top).astype(jnp.bfloat16)
                rescale = jnp.exp(old_top - new_top)
                mixed[i] = mixed[i] * rescale + jnp.dot(value_all[j], powered, preferred_element_type=jnp.float32)
                top[i] = new_top

            return carry

        lax.fori_loop(0, 4, pair, 0)
        if last:
            outs[i][...] = (mixed[i, 0:64] / mixed[i, 64:65]).astype(jnp.bfloat16)


def attend(queries, own_sides, sides, state, last):
    rows = queries[0].shape[1]
    first = state is None
    shapes = [(4, 1, rows), (4, 80, rows)]
    args = list(queries) + [own_sides, sides] + ([] if first else list(state))
    scratch = []
    if last:
        out = [jax.ShapeDtypeStruct((64, rows), jnp.bfloat16)] * 4
        scratch = [pltpu.VMEM(s, jnp.float32) for s in shapes]
    else:
        out = [jax.ShapeDtypeStruct(s, jnp.float32) for s in shapes]
    scratch += [
        pltpu.VMEM((4, 1, rows), jnp.float32),
        pltpu.VMEM((4, rows, 64), jnp.bfloat16),
        pltpu.VMEM((4, 80, rows), jnp.bfloat16),
        pltpu.VMEM((4, rows, 1), jnp.float32),
        pltpu.SMEM((4,), jnp.float32),
        pltpu.SMEM((4,), jnp.float32),
        pltpu.SMEM((4,), jnp.float32),
        pltpu.SMEM((4,), jnp.float32),
    ]

    def body(*refs):
        attend_body(first, last, *refs)

    return pl.pallas_call(
        body,
        out_shape=out,
        in_specs=[VMEM] * len(args),
        out_specs=[VMEM] * len(out),
        scratch_shapes=scratch,
        compiler_params=params(16),
    )(*args)


def gather_body(place, first, second, third, fourth, out):
    y = place[0]
    for d, chunk in enumerate((first, second, third, fourth)):
        out[lax.rem(y - d + 4, 4)] = chunk[...]


def gather_heads(place, chunks):
    rows = chunks[0].shape[1]
    return pl.pallas_call(
        gather_body,
        name="gather_heads",
        out_shape=jax.ShapeDtypeStruct((4, 64, rows), jnp.bfloat16),
        in_specs=[SMEM] + [VMEM] * 4,
        out_specs=VMEM,
        compiler_params=params(8),
    )(place, *chunks)


def columns(index):
    return pl.ds(pl.multiple_of(index * 256, 256), 256)


def feed_body(place, *refs):
    parts, mixed, outers, (gain, w_up, w_down), outs, scratch = (
        refs[:4], refs[4:8], refs[8:12], refs[12:15], refs[15:20], refs[20:]
    )
    far_keep, far_give, near_keep, near_give, share = outs
    features, residual, normed = scratch
    x, c = place[1], place[2]
    rows = parts[0].shape[0]
    for source, at in zip(parts, group_orders(x, c)):
        features[at] = source[...]
    attn = jnp.zeros((rows, 1024), jnp.float32)
    for heads, outer in zip(mixed, outers):
        turned = heads[...].reshape(256, rows).astype(jnp.float32).T.astype(jnp.bfloat16)
        attn = attn + jnp.dot(turned, outer[...], preferred_element_type=jnp.float32)
    total = jnp.zeros((rows, 1), jnp.float32)
    for b in range(4):
        part = features[b].astype(jnp.float32) + attn[:, 256 * b : 256 * (b + 1)]
        residual[b] = part
        total = total + jnp.sum(part * part, axis=-1, keepdims=True)
    scale = lax.rsqrt(total * (1.0 / 1024) + epsilon)
    for b in range(4):
        at = slice(256 * b, 256 * (b + 1))
        normed[:, at] = (residual[b] * scale * gain[:, at]).astype(jnp.bfloat16)
    share[...] = residual[2 * x + c]
    raised = jnp.dot(normed[...], w_up[...], preferred_element_type=jnp.float32)
    hidden = (raised * (1.0 + lax.erf(raised * 0.7071067811865476)) * 0.5).astype(jnp.bfloat16)
    near_at, pair_at, far_at, both_at = group_orders(x, c)
    for out, at in ((far_give, both_at), (far_keep, far_at), (near_give, pair_at), (near_keep, near_at)):
        out[...] = jnp.dot(hidden, w_down[:, columns(at)], preferred_element_type=jnp.float32).astype(jnp.bfloat16)


def feed(place, parts, mixed, outers, gain, w_up, w_down):
    rows = parts[0].shape[0]
    return pl.pallas_call(
        feed_body,
        name="feed",
        out_shape=[jax.ShapeDtypeStruct((rows, 256), jnp.bfloat16)] * 4
        + [jax.ShapeDtypeStruct((rows, 256), jnp.float32)],
        in_specs=[SMEM] + [VMEM] * 15,
        out_specs=[VMEM] * 5,
        scratch_shapes=[
            pltpu.VMEM((4, rows, 256), jnp.bfloat16),
            pltpu.VMEM((4, rows, 256), jnp.float32),
            pltpu.VMEM((rows, 1024), jnp.bfloat16),
        ],
        compiler_params=params(32),
    )(place, *parts, *mixed, *outers, gain, w_up, w_down)


def everyone(block):
    far = send(block, to_chip)
    return [block, send(block, to_core), far, send(far, to_core)]


def layer(hit_features, segment, norm1_gain, w_qkv, w_out, norm2_gain, w_up, w_down):
    place = jnp.stack([lax.axis_index("y"), lax.axis_index("xl"), lax.axis_index("core")]).astype(jnp.int32)
    parts = everyone(hit_features)
    weights, parts[0], tags = stage(w_qkv, hit_features, segment[None, :])
    made = project(place, parts, tags, norm1_gain[None, :], weights)
    arrived = [made[4]]
    for d in range(1, 4):
        arrived.append(send(made[4 + d], to_y(d)))
    w_late, _ = lax.optimization_barrier((w_out, made[4]))
    w_far = send(w_late, to_chip)
    sides = pack(arrived)
    lower, upper = send(sides, to_super(1)), send(sides, to_super(-1))
    late = lax.optimization_barrier((*made[1:4], sides))
    queries = [made[0]] + [send(late[d - 1], to_y(d)) for d in range(1, 4)]
    state = attend(queries, sides, sides, None, False)
    w_own, w_far, *state = lax.optimization_barrier((w_late, w_far, *state))
    outers = [w_own, send(w_own, to_core), w_far, send(w_far, to_core)]
    state = attend(queries, sides, lower, state, False)
    mixed = attend(queries, sides, upper, state, True)
    chunks = [mixed[0]] + [None] * 3
    for d in range(1, 4):
        chunks[(4 - d) % 4] = send(mixed[d], to_y(-d))
    heads = everyone(gather_heads(place, chunks))
    far_keep, far_give, near_keep, near_give, share = feed(
        place, parts, heads, outers, norm2_gain[None, :], w_up, w_down
    )
    summed = far_keep.astype(jnp.float32) + send(far_give, to_core).astype(jnp.float32)
    got = send(summed.astype(jnp.bfloat16), to_chip)
    own = share + near_keep.astype(jnp.float32) + send(near_give, to_core).astype(jnp.float32)
    return (own + got.astype(jnp.float32)).astype(jnp.bfloat16)


def solution(mesh):
    fine = Mesh(mesh.devices.reshape(SIZES), AXES)
    return jax.shard_map(
        layer,
        mesh=fine,
        in_specs=(
            P(CTX, TP),
            P(CTX),
            P(),
            P(None, None, TP),
            P(TP, None),
            P(),
            P(None, TP),
            P(TP, None),
        ),
        out_specs=P(CTX, TP),
        check_vma=False,
    )
```

```python
import jax
import jax.numpy as jnp
from jax import lax
from jax.experimental import pallas as pl
from jax.experimental.pallas import tpu as pltpu
from jax.sharding import Mesh, PartitionSpec as P


HEAD_DIM = 64
epsilon = 1e-05
neg_fill = -1e30
AXES = ("z", "xh", "y", "xl", "core")
CTX = ("z", "xh", "y")
TP = ("xl", "core")
SIZES = (8, 2, 4, 2, 2)
TAG_ROWS = 8


def flat(place):
    index = 0
    for size, at in zip(SIZES, place):
        index = index * size + at
    return index


def every_place():
    for index in range(256):
        place = []
        for size in reversed(SIZES):
            place.append(index % size)
            index //= size
        yield tuple(reversed(place))


def send(block, move):
    route = []
    for place in every_place():
        target = move(*place)
        if target is not None:
            route.append((flat(place), flat(target)))
    return lax.ppermute(block, AXES, route)


def to_y(distance):
    return lambda z, xh, y, xl, c: (z, xh, (y + distance) % 4, xl, c)


def to_super(distance):
    def move(z, xh, y, xl, c):
        at = 2 * z + xh + distance
        return (at // 2, at % 2, y, xl, c) if 0 <= at < 16 else None

    return move


def to_core(z, xh, y, xl, c):
    return (z, xh, y, xl, 1 - c)


def to_chip(z, xh, y, xl, c):
    return (z, xh, y, 1 - xl, c)


def params(mib):
    return pltpu.CompilerParams(vmem_limit_bytes=mib << 20)


SMEM = pl.BlockSpec(memory_space=pltpu.SMEM)
VMEM = pl.BlockSpec(memory_space=pltpu.VMEM)
HBM = pl.BlockSpec(memory_space=pltpu.HBM)


def group_orders(x, c):
    return (2 * x + c, 2 * x + 1 - c, 2 * (1 - x) + c, 2 * (1 - x) + 1 - c)


def stage_body(weights, own, segment, gain, weights_out, own_out, tags, gain_out, sems):
    copies = [
        pltpu.make_async_copy(weights, weights_out, sems.at[0]),
        pltpu.make_async_copy(own, own_out, sems.at[1]),
    ]
    for copy in copies:
        copy.start()
    tag = (segment[...] + 1).astype(jnp.float32)
    tags[...] = jnp.broadcast_to(tag, tags.shape).astype(jnp.bfloat16)
    gain_out[...] = gain[...]
    for copy in copies:
        copy.wait()


def stage(weights, own, segment, gain):
    return pl.pallas_call(
        stage_body,
        name="stage",
        out_shape=[
            jax.ShapeDtypeStruct(weights.shape, weights.dtype),
            jax.ShapeDtypeStruct(own.shape, own.dtype),
            jax.ShapeDtypeStruct((TAG_ROWS, own.shape[0]), jnp.bfloat16),
            jax.ShapeDtypeStruct(gain.shape, gain.dtype),
        ],
        in_specs=[HBM, HBM, VMEM, VMEM],
        out_specs=[VMEM] * 4,
        scratch_shapes=[pltpu.SemaphoreType.DMA((2,))],
        compiler_params=params(8),
    )(weights, own, segment, gain)


def project_body(place, own, near, far, both, tags, gain, weights, *rest):
    queries, sides, (features, normed, heads) = rest[:4], rest[4:8], rest[8:]
    y = place[0]
    rows = own.shape[0]
    total = jnp.zeros((rows, 1), jnp.float32)
    for source, at in zip((own, near, far, both), group_orders(place[1], place[2])):
        part = source[...].astype(jnp.float32)
        total = total + jnp.sum(part * part, axis=-1, keepdims=True)
        features[at] = source[...]
    scale = lax.rsqrt(total * (1.0 / 1024) + epsilon)
    for j in range(4):
        at = slice(256 * j, 256 * (j + 1))
        normed[:, at] = (features[j].astype(jnp.float32) * scale * gain[:, at]).astype(jnp.bfloat16)
    for c in range(3):
        out = jnp.dot(normed[...], weights[c], preferred_element_type=jnp.float32)
        if c == 0:
            out = out * HEAD_DIM ** (-0.5)
        turned = out.T.astype(jnp.bfloat16)
        for h in range(4):
            heads[h, 64 * c : 64 * (c + 1), :] = turned[64 * h : 64 * (h + 1)]
    for d in range(4):
        h = lax.rem(y + d, 4)
        queries[d][...] = heads[h, 0:64, :]
        sides[d][0:128, :] = heads[h, 64:192, :]
        sides[d][128 : 128 + TAG_ROWS, :] = tags[...]


def project(place, parts, tags, gain, weights):
    rows = parts[0].shape[0]
    return pl.pallas_call(
        project_body,
        name="project",
        out_shape=[jax.ShapeDtypeStruct((64, rows), jnp.bfloat16)] * 4
        + [jax.ShapeDtypeStruct((128 + TAG_ROWS, rows), jnp.bfloat16)] * 4,
        in_specs=[SMEM] + [VMEM] * 7,
        out_specs=[VMEM] * 8,
        scratch_shapes=[
            pltpu.VMEM((4, rows, 256), jnp.bfloat16),
            pltpu.VMEM((rows, 1024), jnp.bfloat16),
            pltpu.VMEM((4, 192, rows), jnp.bfloat16),
        ],
        compiler_params=params(20),
    )(place, *parts, tags, gain, weights)


def pack_body(first, second, third, fourth, out):
    for d, source in enumerate((first, second, third, fourth)):
        out[d] = source[...]


def pack(payloads):
    rows = payloads[0].shape[1]
    return pl.pallas_call(
        pack_body,
        name="pack",
        out_shape=jax.ShapeDtypeStruct((4, 128 + TAG_ROWS, rows), jnp.bfloat16),
        in_specs=[VMEM] * 4,
        out_specs=VMEM,
        compiler_params=params(8),
    )(*payloads)


def attend_body(first, last, *refs):
    queries, own_sides, sides, refs = refs[:4], refs[4], refs[5], refs[6:]
    if not first:
        top_in, mixed_in = refs[:2]
        refs = refs[2:]
    if last:
        outs, refs = refs[:4], refs[4:]
    top, mixed = refs[:2]
    query_tag, key_all, value_all, key_tag, query_low, query_high, key_low, key_high = refs[2:]
    rows = sides.shape[2]
    for i in range(4):
        tag = own_sides[i, 128 : 128 + TAG_ROWS, :].astype(jnp.float32)[0:1]
        query_tag[i] = tag
        query_low[i] = jnp.min(tag)
        query_high[i] = jnp.max(tag)
    all_low = jnp.minimum(jnp.minimum(query_low[0], query_low[1]), jnp.minimum(query_low[2], query_low[3]))
    all_high = jnp.maximum(jnp.maximum(query_high[0], query_high[1]), jnp.maximum(query_high[2], query_high[3]))
    for j in range(4):
        tags = sides[j, 128 : 128 + TAG_ROWS, :].astype(jnp.float32)
        low, high = jnp.min(tags), jnp.max(tags)
        key_low[j] = low
        key_high[j] = high

        @pl.when((all_low <= high) & (low <= all_high))
        def _():
            key_all[j] = sides[j, 0:64, :].astype(jnp.float32).T.astype(jnp.bfloat16)
            value_all[j, 0:64] = sides[j, 64:128, :]
            value_all[j, 64:80] = jnp.ones((16, rows), jnp.bfloat16)
            key_tag[j] = tags.T[:, 0:1]

    if first:
        top[...] = jnp.full(top.shape, neg_fill, jnp.float32)
        mixed[...] = jnp.zeros(mixed.shape, jnp.float32)
    else:
        top[...] = top_in[...]
        mixed[...] = mixed_in[...]

    for i in range(4):

        def pair(j, carry):
            meets = (query_low[i] <= key_high[j]) & (key_low[j] <= query_high[i])

            @pl.when(meets)
            def _():
                scores = jnp.dot(key_all[j], queries[i][...], preferred_element_type=jnp.float32)
                masked = jnp.where(key_tag[j] == query_tag[i], scores, 2 * neg_fill)
                old_top = top[i]
                new_top = jnp.maximum(old_top, jnp.max(masked, axis=0, keepdims=True))
                powered = jnp.exp(masked - new_top).astype(jnp.bfloat16)
                rescale = jnp.exp(old_top - new_top)
                mixed[i] = mixed[i] * rescale + jnp.dot(value_all[j], powered, preferred_element_type=jnp.float32)
                top[i] = new_top

            return carry

        lax.fori_loop(0, 4, pair, 0)
        if last:
            outs[i][...] = (mixed[i, 0:64] / mixed[i, 64:65]).astype(jnp.bfloat16)


def attend(queries, own_sides, sides, state, last):
    rows = queries[0].shape[1]
    first = state is None
    shapes = [(4, 1, rows), (4, 80, rows)]
    args = list(queries) + [own_sides, sides] + ([] if first else list(state))
    scratch = []
    if last:
        out = [jax.ShapeDtypeStruct((64, rows), jnp.bfloat16)] * 4
        scratch = [pltpu.VMEM(s, jnp.float32) for s in shapes]
    else:
        out = [jax.ShapeDtypeStruct(s, jnp.float32) for s in shapes]
    scratch += [
        pltpu.VMEM((4, 1, rows), jnp.float32),
        pltpu.VMEM((4, rows, 64), jnp.bfloat16),
        pltpu.VMEM((4, 80, rows), jnp.bfloat16),
        pltpu.VMEM((4, rows, 1), jnp.float32),
        pltpu.SMEM((4,), jnp.float32),
        pltpu.SMEM((4,), jnp.float32),
        pltpu.SMEM((4,), jnp.float32),
        pltpu.SMEM((4,), jnp.float32),
    ]

    def body(*refs):
        attend_body(first, last, *refs)

    return pl.pallas_call(
        body,
        out_shape=out,
        in_specs=[VMEM] * len(args),
        out_specs=[VMEM] * len(out),
        scratch_shapes=scratch,
        compiler_params=params(16),
    )(*args)


def gather_body(place, first, second, third, fourth, out):
    y = place[0]
    for d, chunk in enumerate((first, second, third, fourth)):
        out[lax.rem(y - d + 4, 4)] = chunk[...]


def gather_heads(place, chunks):
    rows = chunks[0].shape[1]
    return pl.pallas_call(
        gather_body,
        name="gather_heads",
        out_shape=jax.ShapeDtypeStruct((4, 64, rows), jnp.bfloat16),
        in_specs=[SMEM] + [VMEM] * 4,
        out_specs=VMEM,
        compiler_params=params(8),
    )(place, *chunks)


def columns(index):
    return pl.ds(pl.multiple_of(index * 256, 256), 256)


def feed_body(place, *refs):
    parts, mixed, outers, (gain, w_up, w_down), outs, scratch = (
        refs[:4], refs[4:8], refs[8:12], refs[12:15], refs[15:20], refs[20:]
    )
    far_keep, far_give, near_keep, near_give, share = outs
    features, residual, normed = scratch
    x, c = place[1], place[2]
    rows = parts[0].shape[0]
    for source, at in zip(parts, group_orders(x, c)):
        features[at] = source[...]
    attn = jnp.zeros((rows, 1024), jnp.float32)
    for heads, outer in zip(mixed, outers):
        turned = heads[...].reshape(256, rows).astype(jnp.float32).T.astype(jnp.bfloat16)
        attn = attn + jnp.dot(turned, outer[...], preferred_element_type=jnp.float32)
    total = jnp.zeros((rows, 1), jnp.float32)
    for b in range(4):
        part = features[b].astype(jnp.float32) + attn[:, 256 * b : 256 * (b + 1)]
        residual[b] = part
        total = total + jnp.sum(part * part, axis=-1, keepdims=True)
    scale = lax.rsqrt(total * (1.0 / 1024) + epsilon)
    for b in range(4):
        at = slice(256 * b, 256 * (b + 1))
        normed[:, at] = (residual[b] * scale * gain[:, at]).astype(jnp.bfloat16)
    share[...] = residual[2 * x + c]
    raised = jnp.dot(normed[...], w_up[...], preferred_element_type=jnp.float32)
    hidden = (raised * (1.0 + lax.erf(raised * 0.7071067811865476)) * 0.5).astype(jnp.bfloat16)
    near_at, pair_at, far_at, both_at = group_orders(x, c)
    for out, at in ((far_give, both_at), (far_keep, far_at), (near_give, pair_at), (near_keep, near_at)):
        out[...] = jnp.dot(hidden, w_down[:, columns(at)], preferred_element_type=jnp.float32).astype(jnp.bfloat16)


def feed(place, parts, mixed, outers, gain, w_up, w_down):
    rows = parts[0].shape[0]
    return pl.pallas_call(
        feed_body,
        name="feed",
        out_shape=[jax.ShapeDtypeStruct((rows, 256), jnp.bfloat16)] * 4
        + [jax.ShapeDtypeStruct((rows, 256), jnp.float32)],
        in_specs=[SMEM] + [VMEM] * 15,
        out_specs=[VMEM] * 5,
        scratch_shapes=[
            pltpu.VMEM((4, rows, 256), jnp.bfloat16),
            pltpu.VMEM((4, rows, 256), jnp.float32),
            pltpu.VMEM((rows, 1024), jnp.bfloat16),
        ],
        compiler_params=params(32),
    )(place, *parts, *mixed, *outers, gain, w_up, w_down)


def everyone(block):
    far = send(block, to_chip)
    both = send(far, to_core)
    return [block, send(block, to_core), far, both]


def layer(hit_features, segment, norm1_gain, w_qkv, w_out, norm2_gain, w_up, w_down):
    place = jnp.stack([lax.axis_index("y"), lax.axis_index("xl"), lax.axis_index("core")]).astype(jnp.int32)
    parts = everyone(hit_features)
    weights, parts[0], tags, gain = stage(w_qkv, hit_features, segment[None, :], norm1_gain[None, :])
    made = project(place, parts, tags, gain, weights)
    arrived = [made[4]]
    for d in range(1, 4):
        arrived.append(send(made[4 + d], to_y(d)))
    w_late, _ = lax.optimization_barrier((w_out, parts[2]))
    w_far = send(w_late, to_chip)
    sides = pack(arrived)
    lower, upper = send(sides, to_super(1)), send(sides, to_super(-1))
    late = lax.optimization_barrier((*made[1:4], sides))
    queries = [made[0]] + [send(late[d - 1], to_y(d)) for d in range(1, 4)]
    state = attend(queries, sides, sides, None, False)
    w_own, w_far, *state = lax.optimization_barrier((w_late, w_far, *state))
    outers = [w_own, send(w_own, to_core), w_far, send(w_far, to_core)]
    state = attend(queries, sides, lower, state, False)
    mixed = attend(queries, sides, upper, state, True)
    chunks = [mixed[0]] + [None] * 3
    for d in range(1, 4):
        chunks[(4 - d) % 4] = send(mixed[d], to_y(-d))
    heads = everyone(gather_heads(place, chunks))
    far_keep, far_give, near_keep, near_give, share = feed(
        place, parts, heads, outers, norm2_gain[None, :], w_up, w_down
    )
    summed = far_keep.astype(jnp.float32) + send(far_give, to_core).astype(jnp.float32)
    got = send(summed.astype(jnp.bfloat16), to_chip)
    own = share + near_keep.astype(jnp.float32) + send(near_give, to_core).astype(jnp.float32)
    return (own + got.astype(jnp.float32)).astype(jnp.bfloat16)


def solution(mesh):
    fine = Mesh(mesh.devices.reshape(SIZES), AXES)
    return jax.shard_map(
        layer,
        mesh=fine,
        in_specs=(
            P(CTX, TP),
            P(CTX),
            P(),
            P(None, None, TP),
            P(TP, None),
            P(),
            P(None, TP),
            P(TP, None),
        ),
        out_specs=P(CTX, TP),
        check_vma=False,
    )
```

```python
import jax
import jax.numpy as jnp
from jax import lax
from jax.experimental import pallas as pl
from jax.experimental.pallas import tpu as pltpu
from jax.sharding import Mesh, PartitionSpec as P


HEAD_DIM = 64
epsilon = 1e-05
neg_fill = -1e30
AXES = ("z", "xh", "y", "xl", "core")
CTX = ("z", "xh", "y")
TP = ("xl", "core")
SIZES = (8, 2, 4, 2, 2)
TAG_ROWS = 8


def flat(place):
    index = 0
    for size, at in zip(SIZES, place):
        index = index * size + at
    return index


def every_place():
    for index in range(256):
        place = []
        for size in reversed(SIZES):
            place.append(index % size)
            index //= size
        yield tuple(reversed(place))


def send(block, move):
    route = []
    for place in every_place():
        target = move(*place)
        if target is not None:
            route.append((flat(place), flat(target)))
    return lax.ppermute(block, AXES, route)


def to_y(distance):
    return lambda z, xh, y, xl, c: (z, xh, (y + distance) % 4, xl, c)


def to_super(distance):
    def move(z, xh, y, xl, c):
        at = 2 * z + xh + distance
        return (at // 2, at % 2, y, xl, c) if 0 <= at < 16 else None

    return move


def to_core(z, xh, y, xl, c):
    return (z, xh, y, xl, 1 - c)


def to_chip(z, xh, y, xl, c):
    return (z, xh, y, 1 - xl, c)


def params(mib):
    return pltpu.CompilerParams(vmem_limit_bytes=mib << 20)


SMEM = pl.BlockSpec(memory_space=pltpu.SMEM)
VMEM = pl.BlockSpec(memory_space=pltpu.VMEM)
HBM = pl.BlockSpec(memory_space=pltpu.HBM)


def group_orders(x, c):
    return (2 * x + c, 2 * x + 1 - c, 2 * (1 - x) + c, 2 * (1 - x) + 1 - c)


def stage_body(weights, own, segment, gain, weights_out, own_out, tags, gain_out, sems):
    copies = [
        pltpu.make_async_copy(weights, weights_out, sems.at[0]),
        pltpu.make_async_copy(own, own_out, sems.at[1]),
    ]
    for copy in copies:
        copy.start()
    tag = (segment[...] + 1).astype(jnp.float32)
    tags[...] = jnp.broadcast_to(tag, tags.shape).astype(jnp.bfloat16)
    gain_out[...] = gain[...]
    for copy in copies:
        copy.wait()


def stage(weights, own, segment, gain):
    return pl.pallas_call(
        stage_body,
        name="stage",
        out_shape=[
            jax.ShapeDtypeStruct(weights.shape, weights.dtype),
            jax.ShapeDtypeStruct(own.shape, own.dtype),
            jax.ShapeDtypeStruct((TAG_ROWS, own.shape[0]), jnp.bfloat16),
            jax.ShapeDtypeStruct(gain.shape, gain.dtype),
        ],
        in_specs=[HBM, HBM, VMEM, VMEM],
        out_specs=[VMEM] * 4,
        scratch_shapes=[pltpu.SemaphoreType.DMA((2,))],
        compiler_params=params(8),
    )(weights, own, segment, gain)


def project_body(place, own, near, far, both, tags, gain, weights, *rest):
    outs, (features, normed, heads) = rest[:4], rest[4:]
    y = place[0]
    rows = own.shape[0]
    total = jnp.zeros((rows, 1), jnp.float32)
    for source, at in zip((own, near, far, both), group_orders(place[1], place[2])):
        part = source[...].astype(jnp.float32)
        total = total + jnp.sum(part * part, axis=-1, keepdims=True)
        features[at] = source[...]
    scale = lax.rsqrt(total * (1.0 / 1024) + epsilon)
    for j in range(4):
        at = slice(256 * j, 256 * (j + 1))
        normed[:, at] = (features[j].astype(jnp.float32) * scale * gain[:, at]).astype(jnp.bfloat16)
    for c in range(3):
        out = jnp.dot(normed[...], weights[c], preferred_element_type=jnp.float32)
        if c == 0:
            out = out * HEAD_DIM ** (-0.5)
        turned = out.T.astype(jnp.bfloat16)
        for h in range(4):
            heads[h, 64 * c : 64 * (c + 1), :] = turned[64 * h : 64 * (h + 1)]
    for d in range(4):
        h = lax.rem(y + d, 4)
        outs[d][0:192, :] = heads[h]
        outs[d][192 : 192 + TAG_ROWS, :] = tags[...]


def project(place, parts, tags, gain, weights):
    rows = parts[0].shape[0]
    return pl.pallas_call(
        project_body,
        name="project",
        out_shape=[jax.ShapeDtypeStruct((192 + TAG_ROWS, rows), jnp.bfloat16)] * 4,
        in_specs=[SMEM] + [VMEM] * 7,
        out_specs=[VMEM] * 4,
        scratch_shapes=[
            pltpu.VMEM((4, rows, 256), jnp.bfloat16),
            pltpu.VMEM((rows, 1024), jnp.bfloat16),
            pltpu.VMEM((4, 192, rows), jnp.bfloat16),
        ],
        compiler_params=params(20),
    )(place, *parts, tags, gain, weights)


def pack_body(first, second, third, fourth, queries, sides):
    for d, source in enumerate((first, second, third, fourth)):
        queries[d] = source[0:64, :]
        sides[d] = source[64 : 192 + TAG_ROWS, :]


def pack(payloads):
    rows = payloads[0].shape[1]
    return pl.pallas_call(
        pack_body,
        name="pack",
        out_shape=[
            jax.ShapeDtypeStruct((4, 64, rows), jnp.bfloat16),
            jax.ShapeDtypeStruct((4, 128 + TAG_ROWS, rows), jnp.bfloat16),
        ],
        in_specs=[VMEM] * 4,
        out_specs=[VMEM] * 2,
        compiler_params=params(8),
    )(*payloads)


def attend_body(first, last, *refs):
    queries, own_sides, sides, refs = refs[0], refs[1], refs[2], refs[3:]
    if not first:
        top_in, mixed_in = refs[:2]
        refs = refs[2:]
    if last:
        outs, refs = refs[:4], refs[4:]
    top, mixed = refs[:2]
    query_tag, key_all, value_all, key_tag, query_low, query_high, key_low, key_high = refs[2:]
    rows = sides.shape[2]
    for i in range(4):
        tag = own_sides[i, 128 : 128 + TAG_ROWS, :].astype(jnp.float32)[0:1]
        query_tag[i] = tag
        query_low[i] = jnp.min(tag)
        query_high[i] = jnp.max(tag)
    all_low = jnp.minimum(jnp.minimum(query_low[0], query_low[1]), jnp.minimum(query_low[2], query_low[3]))
    all_high = jnp.maximum(jnp.maximum(query_high[0], query_high[1]), jnp.maximum(query_high[2], query_high[3]))
    for j in range(4):
        tags = sides[j, 128 : 128 + TAG_ROWS, :].astype(jnp.float32)
        low, high = jnp.min(tags), jnp.max(tags)
        key_low[j] = low
        key_high[j] = high

        @pl.when((all_low <= high) & (low <= all_high))
        def _():
            key_all[j] = sides[j, 0:64, :].astype(jnp.float32).T.astype(jnp.bfloat16)
            value_all[j, 0:64] = sides[j, 64:128, :]
            value_all[j, 64:80] = jnp.ones((16, rows), jnp.bfloat16)
            key_tag[j] = tags.T[:, 0:1]

    if first:
        top[...] = jnp.full(top.shape, neg_fill, jnp.float32)
        mixed[...] = jnp.zeros(mixed.shape, jnp.float32)
    else:
        top[...] = top_in[...]
        mixed[...] = mixed_in[...]

    for i in range(4):

        def pair(j, carry):
            meets = (query_low[i] <= key_high[j]) & (key_low[j] <= query_high[i])

            @pl.when(meets)
            def _():
                scores = jnp.dot(key_all[j], queries[i], preferred_element_type=jnp.float32)
                masked = jnp.where(key_tag[j] == query_tag[i], scores, 2 * neg_fill)
                old_top = top[i]
                new_top = jnp.maximum(old_top, jnp.max(masked, axis=0, keepdims=True))
                powered = jnp.exp(masked - new_top).astype(jnp.bfloat16)
                rescale = jnp.exp(old_top - new_top)
                mixed[i] = mixed[i] * rescale + jnp.dot(value_all[j], powered, preferred_element_type=jnp.float32)
                top[i] = new_top

            return carry

        lax.fori_loop(0, 4, pair, 0)
        if last:
            outs[i][...] = (mixed[i, 0:64] / mixed[i, 64:65]).astype(jnp.bfloat16)


def attend(queries, own_sides, sides, state, last):
    rows = sides.shape[2]
    first = state is None
    shapes = [(4, 1, rows), (4, 80, rows)]
    args = [queries, own_sides, sides] + ([] if first else list(state))
    scratch = []
    if last:
        out = [jax.ShapeDtypeStruct((64, rows), jnp.bfloat16)] * 4
        scratch = [pltpu.VMEM(s, jnp.float32) for s in shapes]
    else:
        out = [jax.ShapeDtypeStruct(s, jnp.float32) for s in shapes]
    scratch += [
        pltpu.VMEM((4, 1, rows), jnp.float32),
        pltpu.VMEM((4, rows, 64), jnp.bfloat16),
        pltpu.VMEM((4, 80, rows), jnp.bfloat16),
        pltpu.VMEM((4, rows, 1), jnp.float32),
        pltpu.SMEM((4,), jnp.float32),
        pltpu.SMEM((4,), jnp.float32),
        pltpu.SMEM((4,), jnp.float32),
        pltpu.SMEM((4,), jnp.float32),
    ]

    def body(*refs):
        attend_body(first, last, *refs)

    return pl.pallas_call(
        body,
        out_shape=out,
        in_specs=[VMEM] * len(args),
        out_specs=[VMEM] * len(out),
        scratch_shapes=scratch,
        compiler_params=params(16),
    )(*args)


def gather_body(place, first, second, third, fourth, out):
    y = place[0]
    for d, chunk in enumerate((first, second, third, fourth)):
        out[lax.rem(y - d + 4, 4)] = chunk[...]


def gather_heads(place, chunks):
    rows = chunks[0].shape[1]
    return pl.pallas_call(
        gather_body,
        name="gather_heads",
        out_shape=jax.ShapeDtypeStruct((4, 64, rows), jnp.bfloat16),
        in_specs=[SMEM] + [VMEM] * 4,
        out_specs=VMEM,
        compiler_params=params(8),
    )(place, *chunks)


def columns(index):
    return pl.ds(pl.multiple_of(index * 256, 256), 256)


def feed_body(place, *refs):
    parts, mixed, outers, (gain, w_up, w_down), outs, scratch = (
        refs[:4], refs[4:8], refs[8:12], refs[12:15], refs[15:20], refs[20:]
    )
    far_keep, far_give, near_keep, near_give, share = outs
    features, residual, normed = scratch
    x, c = place[1], place[2]
    rows = parts[0].shape[0]
    for source, at in zip(parts, group_orders(x, c)):
        features[at] = source[...]
    attn = jnp.zeros((rows, 1024), jnp.float32)
    for heads, outer in zip(mixed, outers):
        turned = heads[...].reshape(256, rows).astype(jnp.float32).T.astype(jnp.bfloat16)
        attn = attn + jnp.dot(turned, outer[...], preferred_element_type=jnp.float32)
    total = jnp.zeros((rows, 1), jnp.float32)
    for b in range(4):
        part = features[b].astype(jnp.float32) + attn[:, 256 * b : 256 * (b + 1)]
        residual[b] = part
        total = total + jnp.sum(part * part, axis=-1, keepdims=True)
    scale = lax.rsqrt(total * (1.0 / 1024) + epsilon)
    for b in range(4):
        at = slice(256 * b, 256 * (b + 1))
        normed[:, at] = (residual[b] * scale * gain[:, at]).astype(jnp.bfloat16)
    share[...] = residual[2 * x + c]
    raised = jnp.dot(normed[...], w_up[...], preferred_element_type=jnp.float32)
    hidden = (raised * (1.0 + lax.erf(raised * 0.7071067811865476)) * 0.5).astype(jnp.bfloat16)
    near_at, pair_at, far_at, both_at = group_orders(x, c)
    for out, at in ((far_give, both_at), (far_keep, far_at), (near_give, pair_at), (near_keep, near_at)):
        out[...] = jnp.dot(hidden, w_down[:, columns(at)], preferred_element_type=jnp.float32).astype(jnp.bfloat16)


def feed(place, parts, mixed, outers, gain, w_up, w_down):
    rows = parts[0].shape[0]
    return pl.pallas_call(
        feed_body,
        name="feed",
        out_shape=[jax.ShapeDtypeStruct((rows, 256), jnp.bfloat16)] * 4
        + [jax.ShapeDtypeStruct((rows, 256), jnp.float32)],
        in_specs=[SMEM] + [VMEM] * 15,
        out_specs=[VMEM] * 5,
        scratch_shapes=[
            pltpu.VMEM((4, rows, 256), jnp.bfloat16),
            pltpu.VMEM((4, rows, 256), jnp.float32),
            pltpu.VMEM((rows, 1024), jnp.bfloat16),
        ],
        compiler_params=params(32),
    )(place, *parts, *mixed, *outers, gain, w_up, w_down)


def everyone(block):
    far = send(block, to_chip)
    both = send(far, to_core)
    return [block, send(block, to_core), far, both]


def layer(hit_features, segment, norm1_gain, w_qkv, w_out, norm2_gain, w_up, w_down):
    place = jnp.stack([lax.axis_index("y"), lax.axis_index("xl"), lax.axis_index("core")]).astype(jnp.int32)
    parts = everyone(hit_features)
    weights, parts[0], tags, gain = stage(w_qkv, hit_features, segment[None, :], norm1_gain[None, :])
    made = project(place, parts, tags, gain, weights)
    arrived = [made[0]]
    for d in range(1, 4):
        arrived.append(send(made[d], to_y(d)))
    w_late, _ = lax.optimization_barrier((w_out, parts[2]))
    w_far = send(w_late, to_chip)
    queries, sides = pack(arrived)
    lower, upper = send(sides, to_super(1)), send(sides, to_super(-1))
    state = attend(queries, sides, sides, None, False)
    state = attend(queries, sides, lower, state, False)
    mixed = attend(queries, sides, upper, state, True)
    chunks = [mixed[0]] + [None] * 3
    for d in range(1, 4):
        chunks[(4 - d) % 4] = send(mixed[d], to_y(-d))
    gathered, w_own, w_far = lax.optimization_barrier((gather_heads(place, chunks), w_late, w_far))
    heads = everyone(gathered)
    outers = [w_own, send(w_own, to_core), w_far, send(w_far, to_core)]
    far_keep, far_give, near_keep, near_give, share = feed(
        place, parts, heads, outers, norm2_gain[None, :], w_up, w_down
    )
    summed = far_keep.astype(jnp.float32) + send(far_give, to_core).astype(jnp.float32)
    got = send(summed.astype(jnp.bfloat16), to_chip)
    own = share + near_keep.astype(jnp.float32) + send(near_give, to_core).astype(jnp.float32)
    return (own + got.astype(jnp.float32)).astype(jnp.bfloat16)


def solution(mesh):
    fine = Mesh(mesh.devices.reshape(SIZES), AXES)
    return jax.shard_map(
        layer,
        mesh=fine,
        in_specs=(
            P(CTX, TP),
            P(CTX),
            P(),
            P(None, None, TP),
            P(TP, None),
            P(),
            P(None, TP),
            P(TP, None),
        ),
        out_specs=P(CTX, TP),
        check_vma=False,
    )
```

```python
import jax
import jax.numpy as jnp
from jax import lax
from jax.experimental import pallas as pl
from jax.experimental.pallas import tpu as pltpu
from jax.sharding import Mesh, PartitionSpec as P


HEAD_DIM = 64
epsilon = 1e-05
neg_fill = -1e30
AXES = ("z", "xh", "y", "xl", "core")
CTX = ("z", "xh", "y")
TP = ("xl", "core")
SIZES = (8, 2, 4, 2, 2)
TAG_ROWS = 8


def flat(place):
    index = 0
    for size, at in zip(SIZES, place):
        index = index * size + at
    return index


def every_place():
    for index in range(256):
        place = []
        for size in reversed(SIZES):
            place.append(index % size)
            index //= size
        yield tuple(reversed(place))


def send(block, move):
    route = []
    for place in every_place():
        target = move(*place)
        if target is not None:
            route.append((flat(place), flat(target)))
    return lax.ppermute(block, AXES, route)


def to_y(distance):
    return lambda z, xh, y, xl, c: (z, xh, (y + distance) % 4, xl, c)


def to_super(distance):
    def move(z, xh, y, xl, c):
        at = 2 * z + xh + distance
        return (at // 2, at % 2, y, xl, c) if 0 <= at < 16 else None

    return move


def to_core(z, xh, y, xl, c):
    return (z, xh, y, xl, 1 - c)


def to_chip(z, xh, y, xl, c):
    return (z, xh, y, 1 - xl, c)


def params(mib):
    return pltpu.CompilerParams(vmem_limit_bytes=mib << 20)


SMEM = pl.BlockSpec(memory_space=pltpu.SMEM)
VMEM = pl.BlockSpec(memory_space=pltpu.VMEM)
HBM = pl.BlockSpec(memory_space=pltpu.HBM)


def group_orders(x, c):
    return (2 * x + c, 2 * x + 1 - c, 2 * (1 - x) + c, 2 * (1 - x) + 1 - c)


def stage_body(weights, own, segment, gain, weights_out, own_out, tags, gain_out, sems):
    copies = [
        pltpu.make_async_copy(weights, weights_out, sems.at[0]),
        pltpu.make_async_copy(own, own_out, sems.at[1]),
    ]
    for copy in copies:
        copy.start()
    tag = (segment[...] + 1).astype(jnp.float32)
    tags[...] = jnp.broadcast_to(tag, tags.shape).astype(jnp.bfloat16)
    gain_out[...] = gain[...]
    for copy in copies:
        copy.wait()


def stage(weights, own, segment, gain):
    return pl.pallas_call(
        stage_body,
        name="stage",
        out_shape=[
            jax.ShapeDtypeStruct(weights.shape, weights.dtype),
            jax.ShapeDtypeStruct(own.shape, own.dtype),
            jax.ShapeDtypeStruct((TAG_ROWS, own.shape[0]), jnp.bfloat16),
            jax.ShapeDtypeStruct(gain.shape, gain.dtype),
        ],
        in_specs=[HBM, HBM, VMEM, VMEM],
        out_specs=[VMEM] * 4,
        scratch_shapes=[pltpu.SemaphoreType.DMA((2,))],
        compiler_params=params(8),
    )(weights, own, segment, gain)


def project_body(place, own, near, far, both, tags, gain, weights, *rest):
    queries, sides, (features, normed, heads) = rest[:4], rest[4:8], rest[8:]
    y = place[0]
    rows = own.shape[0]
    total = jnp.zeros((rows, 1), jnp.float32)
    for source, at in zip((own, near, far, both), group_orders(place[1], place[2])):
        part = source[...].astype(jnp.float32)
        total = total + jnp.sum(part * part, axis=-1, keepdims=True)
        features[at] = source[...]
    scale = lax.rsqrt(total * (1.0 / 1024) + epsilon)
    for j in range(4):
        at = slice(256 * j, 256 * (j + 1))
        normed[:, at] = (features[j].astype(jnp.float32) * scale * gain[:, at]).astype(jnp.bfloat16)
    for c in range(3):
        out = jnp.dot(normed[...], weights[c], preferred_element_type=jnp.float32)
        if c == 0:
            out = out * HEAD_DIM ** (-0.5)
        turned = out.T.astype(jnp.bfloat16)
        for h in range(4):
            heads[h, 64 * c : 64 * (c + 1), :] = turned[64 * h : 64 * (h + 1)]
    for d in range(4):
        h = lax.rem(y + d, 4)
        queries[d][...] = heads[h, 0:64, :]
        sides[d][0:128, :] = heads[h, 64:192, :]
        sides[d][128 : 128 + TAG_ROWS, :] = tags[...]


def project(place, parts, tags, gain, weights):
    rows = parts[0].shape[0]
    return pl.pallas_call(
        project_body,
        name="project",
        out_shape=[jax.ShapeDtypeStruct((64, rows), jnp.bfloat16)] * 4
        + [jax.ShapeDtypeStruct((128 + TAG_ROWS, rows), jnp.bfloat16)] * 4,
        in_specs=[SMEM] + [VMEM] * 7,
        out_specs=[VMEM] * 8,
        scratch_shapes=[
            pltpu.VMEM((4, rows, 256), jnp.bfloat16),
            pltpu.VMEM((rows, 1024), jnp.bfloat16),
            pltpu.VMEM((4, 192, rows), jnp.bfloat16),
        ],
        compiler_params=params(20),
    )(place, *parts, tags, gain, weights)


def pack_body(first, second, third, fourth, out):
    for d, source in enumerate((first, second, third, fourth)):
        out[d] = source[...]


def pack(payloads):
    rows = payloads[0].shape[1]
    return pl.pallas_call(
        pack_body,
        name="pack",
        out_shape=jax.ShapeDtypeStruct((4, 128 + TAG_ROWS, rows), jnp.bfloat16),
        in_specs=[VMEM] * 4,
        out_specs=VMEM,
        compiler_params=params(8),
    )(*payloads)


def attend_body(first, last, *refs):
    queries, own_sides, sides, refs = refs[:4], refs[4], refs[5], refs[6:]
    if not first:
        top_in, mixed_in = refs[:2]
        refs = refs[2:]
    if last:
        outs, refs = refs[:4], refs[4:]
    top, mixed = refs[:2]
    query_tag, key_all, value_all, key_tag, query_low, query_high, key_low, key_high = refs[2:]
    rows = sides.shape[2]
    for i in range(4):
        tag = own_sides[i, 128 : 128 + TAG_ROWS, :].astype(jnp.float32)[0:1]
        query_tag[i] = tag
        query_low[i] = jnp.min(tag)
        query_high[i] = jnp.max(tag)
    all_low = jnp.minimum(jnp.minimum(query_low[0], query_low[1]), jnp.minimum(query_low[2], query_low[3]))
    all_high = jnp.maximum(jnp.maximum(query_high[0], query_high[1]), jnp.maximum(query_high[2], query_high[3]))
    for j in range(4):
        tags = sides[j, 128 : 128 + TAG_ROWS, :].astype(jnp.float32)
        low, high = jnp.min(tags), jnp.max(tags)
        key_low[j] = low
        key_high[j] = high

        @pl.when((all_low <= high) & (low <= all_high))
        def _():
            key_all[j] = sides[j, 0:64, :].astype(jnp.float32).T.astype(jnp.bfloat16)
            value_all[j, 0:64] = sides[j, 64:128, :]
            value_all[j, 64:80] = jnp.ones((16, rows), jnp.bfloat16)
            key_tag[j] = tags.T[:, 0:1]

    if first:
        top[...] = jnp.full(top.shape, neg_fill, jnp.float32)
        mixed[...] = jnp.zeros(mixed.shape, jnp.float32)
    else:
        top[...] = top_in[...]
        mixed[...] = mixed_in[...]

    for i in range(4):

        def pair(j, carry):
            meets = (query_low[i] <= key_high[j]) & (key_low[j] <= query_high[i])

            @pl.when(meets)
            def _():
                scores = jnp.dot(key_all[j], queries[i][...], preferred_element_type=jnp.float32)
                masked = jnp.where(key_tag[j] == query_tag[i], scores, 2 * neg_fill)
                old_top = top[i]
                new_top = jnp.maximum(old_top, jnp.max(masked, axis=0, keepdims=True))
                powered = jnp.exp(masked - new_top).astype(jnp.bfloat16)
                rescale = jnp.exp(old_top - new_top)
                mixed[i] = mixed[i] * rescale + jnp.dot(value_all[j], powered, preferred_element_type=jnp.float32)
                top[i] = new_top

            return carry

        lax.fori_loop(0, 4, pair, 0)
        if last:
            outs[i][...] = (mixed[i, 0:64] / mixed[i, 64:65]).astype(jnp.bfloat16)


def attend(queries, own_sides, sides, state, last):
    rows = queries[0].shape[1]
    first = state is None
    shapes = [(4, 1, rows), (4, 80, rows)]
    args = list(queries) + [own_sides, sides] + ([] if first else list(state))
    scratch = []
    if last:
        out = [jax.ShapeDtypeStruct((64, rows), jnp.bfloat16)] * 4
        scratch = [pltpu.VMEM(s, jnp.float32) for s in shapes]
    else:
        out = [jax.ShapeDtypeStruct(s, jnp.float32) for s in shapes]
    scratch += [
        pltpu.VMEM((4, 1, rows), jnp.float32),
        pltpu.VMEM((4, rows, 64), jnp.bfloat16),
        pltpu.VMEM((4, 80, rows), jnp.bfloat16),
        pltpu.VMEM((4, rows, 1), jnp.float32),
        pltpu.SMEM((4,), jnp.float32),
        pltpu.SMEM((4,), jnp.float32),
        pltpu.SMEM((4,), jnp.float32),
        pltpu.SMEM((4,), jnp.float32),
    ]

    def body(*refs):
        attend_body(first, last, *refs)

    return pl.pallas_call(
        body,
        out_shape=out,
        in_specs=[VMEM] * len(args),
        out_specs=[VMEM] * len(out),
        scratch_shapes=scratch,
        compiler_params=params(16),
    )(*args)


def gather_body(place, first, second, third, fourth, out):
    y = place[0]
    for d, chunk in enumerate((first, second, third, fourth)):
        out[lax.rem(y - d + 4, 4)] = chunk[...]


def gather_heads(place, chunks):
    rows = chunks[0].shape[1]
    return pl.pallas_call(
        gather_body,
        name="gather_heads",
        out_shape=jax.ShapeDtypeStruct((4, 64, rows), jnp.bfloat16),
        in_specs=[SMEM] + [VMEM] * 4,
        out_specs=VMEM,
        compiler_params=params(8),
    )(place, *chunks)


def columns(index):
    return pl.ds(pl.multiple_of(index * 256, 256), 256)


def feed_body(place, *refs):
    parts, mixed, outers, (gain, w_up, w_down), outs, scratch = (
        refs[:4], refs[4:8], refs[8:12], refs[12:15], refs[15:20], refs[20:]
    )
    far_keep, far_give, near_keep, near_give, share = outs
    features, residual, normed = scratch
    x, c = place[1], place[2]
    rows = parts[0].shape[0]
    for source, at in zip(parts, group_orders(x, c)):
        features[at] = source[...]
    attn = jnp.zeros((rows, 1024), jnp.float32)
    for heads, outer in zip(mixed, outers):
        turned = heads[...].reshape(256, rows).astype(jnp.float32).T.astype(jnp.bfloat16)
        attn = attn + jnp.dot(turned, outer[...], preferred_element_type=jnp.float32)
    total = jnp.zeros((rows, 1), jnp.float32)
    for b in range(4):
        part = features[b].astype(jnp.float32) + attn[:, 256 * b : 256 * (b + 1)]
        residual[b] = part
        total = total + jnp.sum(part * part, axis=-1, keepdims=True)
    scale = lax.rsqrt(total * (1.0 / 1024) + epsilon)
    for b in range(4):
        at = slice(256 * b, 256 * (b + 1))
        normed[:, at] = (residual[b] * scale * gain[:, at]).astype(jnp.bfloat16)
    share[...] = residual[2 * x + c]
    raised = jnp.dot(normed[...], w_up[...], preferred_element_type=jnp.float32)
    hidden = (raised * (1.0 + lax.erf(raised * 0.7071067811865476)) * 0.5).astype(jnp.bfloat16)
    near_at, pair_at, far_at, both_at = group_orders(x, c)
    for out, at in ((far_give, both_at), (far_keep, far_at), (near_give, pair_at), (near_keep, near_at)):
        out[...] = jnp.dot(hidden, w_down[:, columns(at)], preferred_element_type=jnp.float32).astype(jnp.bfloat16)


def feed(place, parts, mixed, outers, gain, w_up, w_down):
    rows = parts[0].shape[0]
    return pl.pallas_call(
        feed_body,
        name="feed",
        out_shape=[jax.ShapeDtypeStruct((rows, 256), jnp.bfloat16)] * 4
        + [jax.ShapeDtypeStruct((rows, 256), jnp.float32)],
        in_specs=[SMEM] + [VMEM] * 15,
        out_specs=[VMEM] * 5,
        scratch_shapes=[
            pltpu.VMEM((4, rows, 256), jnp.bfloat16),
            pltpu.VMEM((4, rows, 256), jnp.float32),
            pltpu.VMEM((rows, 1024), jnp.bfloat16),
        ],
        compiler_params=params(32),
    )(place, *parts, *mixed, *outers, gain, w_up, w_down)


def everyone(block):
    far = send(block, to_chip)
    both = send(far, to_core)
    return [block, send(block, to_core), far, both]


def layer(hit_features, segment, norm1_gain, w_qkv, w_out, norm2_gain, w_up, w_down):
    place = jnp.stack([lax.axis_index("y"), lax.axis_index("xl"), lax.axis_index("core")]).astype(jnp.int32)
    parts = everyone(hit_features)
    weights, parts[0], tags, gain = stage(w_qkv, hit_features, segment[None, :], norm1_gain[None, :])
    made = project(place, parts, tags, gain, weights)
    arrived = [made[4]]
    for d in range(1, 4):
        arrived.append(send(made[4 + d], to_y(d)))
    w_late, _ = lax.optimization_barrier((w_out, parts[2]))
    w_far = send(w_late, to_chip)
    sides = pack(arrived)
    lower = send(sides, to_super(1))
    upper = send(sides, to_super(-1))
    late = lax.optimization_barrier((*made[1:4], sides))
    queries = [made[0]]
    for d in range(1, 4):
        queries.append(send(late[d - 1], to_y(d)))
    state = attend(queries, sides, sides, None, False)
    state = attend(queries, sides, lower, state, False)
    mixed = attend(queries, sides, upper, state, True)
    chunks = [mixed[0]] + [None] * 3
    for d in range(1, 4):
        chunks[(4 - d) % 4] = send(mixed[d], to_y(-d))
    gathered, w_own, w_far = lax.optimization_barrier((gather_heads(place, chunks), w_late, w_far))
    heads = everyone(gathered)
    outers = [w_own, send(w_own, to_core), w_far, send(w_far, to_core)]
    far_keep, far_give, near_keep, near_give, share = feed(
        place, parts, heads, outers, norm2_gain[None, :], w_up, w_down
    )
    summed = far_keep.astype(jnp.float32) + send(far_give, to_core).astype(jnp.float32)
    got = send(summed.astype(jnp.bfloat16), to_chip)
    own = share + near_keep.astype(jnp.float32) + send(near_give, to_core).astype(jnp.float32)
    return (own + got.astype(jnp.float32)).astype(jnp.bfloat16)


def solution(mesh):
    fine = Mesh(mesh.devices.reshape(SIZES), AXES)
    return jax.shard_map(
        layer,
        mesh=fine,
        in_specs=(
            P(CTX, TP),
            P(CTX),
            P(),
            P(None, None, TP),
            P(TP, None),
            P(),
            P(None, TP),
            P(TP, None),
        ),
        out_specs=P(CTX, TP),
        check_vma=False,
    )
```
